512 devices in a mesh: row: 16 (over z, core), col: 32 (over x, y).
Axes of the slice: x: 4, y: 8, z: 8, core: 2. Of those that a mesh axis runs over, the one named last changes fastest.
Arguments:
- strip: float32 [20480, 128], P('row'), may hold values from -6 to 6
- block_below: float32 [64, 64], replicated, may hold values from -1 to 1
- inverse_first: float32 [64, 64], replicated, may hold values from -0.5 to 1.5, as said below
- inverse_second: float32 [64, 64], replicated, may hold values from -0.5 to 1.5, as said below
- cotangent: float32 [20480, 20480], P('row', 'col'), may hold values from -0.0390625 to 0.0390625
Outputs:
- strip_grad: float32 [20480, 128], P('row')
The draws below stay inside these ranges and needn't reach their ends.
Inputs may be any that keep to these rules, and one draw needn't show every extreme that they name: inverse_first is lower triangular with its diagonal in 0.5 to 1.5. inverse_second is lower triangular with its diagonal in 0.5 to 1.5.
All inputs are finite; a program needn't handle non-finite values.
Results may differ from the reference program's by a relative error of at most 0.00007.
Values sent between devices are 32-bit elements; how exact they have to be, the bound alone decides.
A program may use at most 64 MiB of HBM per device.

```python
import jax
import jax.numpy as jnp
from jax import lax

M = 20480
PANEL = 64
STRIP = 128


def triangle_draw(key):
    diag_key, off_key = jax.random.split(key)
    diagonal = jax.random.uniform(diag_key, (PANEL, PANEL), jnp.float32, 0.5, 1.5)
    offdiag = jnp.clip(0.1 * jax.random.normal(off_key, (PANEL, PANEL), jnp.float32), -0.5, 0.5)
    rows_index = jnp.arange(PANEL)[:, None]
    cols_index = jnp.arange(PANEL)[None, :]
    return jnp.where(rows_index == cols_index, diagonal, jnp.where(rows_index > cols_index, offdiag, 0.0))


def draw_inverse_first(key, part):
    return triangle_draw(jax.random.fold_in(key, 11))


def draw_inverse_second(key, part):
    return triangle_draw(jax.random.fold_in(key, 12))


def shard_levels(stream_key, shape, cuts, low, high):
    def one(dim, shards_of):
        heights = jax.random.uniform(jax.random.fold_in(jax.random.fold_in(stream_key, 6), dim), (shards_of,), jnp.float32, low / len(cuts), high / len(cuts))
        return jnp.repeat(jnp.exp(heights), shape[dim] // shards_of).reshape((-1,) + (1,) * (len(shape) - dim - 1))

    gain = one(*cuts[0])
    for cut in cuts[1:]:
        gain = gain * one(*cut)
    return gain


def scatter_about(key, shape, width, most, shards=(), kind=jnp.bfloat16):
    factor_of = shard_levels(key, shape, shards, -0.22, 0.18) if shards else 1.0
    entries = jax.random.normal(key, shape, jnp.float32) * width * factor_of
    return jnp.minimum(jnp.maximum(entries, -most), most).astype(kind)


def setup_inputs(seed: int = 0) -> dict:
    key_list = jax.random.split(jax.random.key(seed), 6)
    return {
        "strip": scatter_about(key_list[0], (M, STRIP), 1.0, 6.0, ((0, 16),), jnp.float32),
        "block_below": scatter_about(key_list[1], (PANEL, PANEL), 0.125, 1.0, (), jnp.float32),
        "inverse_first": draw_inverse_first(jax.random.fold_in(key_list[5], 71), 0),
        "inverse_second": draw_inverse_second(jax.random.fold_in(key_list[5], 71), 0),
        "cotangent": scatter_about(key_list[4], (M, M), M ** -0.5, 0.0390625, ((0, 16), (1, 32)), jnp.float32),
    }


def mul(left, right):
    return jnp.dot(left, right, precision=lax.Precision.HIGHEST, preferred_element_type=jnp.float32)


def reference(strip, block_below, inverse_first, inverse_second, cotangent):
    lower_first = mul(strip[:, :PANEL], inverse_first.T)
    left_block = mul(block_below, inverse_first.T)
    updated = strip[:, PANEL:] - mul(lower_first, left_block.T)
    lower_second = mul(updated, inverse_second.T)
    lower = jnp.concatenate([lower_first, lower_second], axis=1)
    transposed = lax.dot_general(cotangent, lower, (((0,), (0,)), ((), ())), precision=lax.Precision.HIGHEST, preferred_element_type=jnp.float32)
    bar_lower = -(mul(cotangent, lower) + transposed)
    bar_updated = mul(bar_lower[:, PANEL:], inverse_second)
    bar_first = bar_lower[:, :PANEL] - mul(bar_updated, left_block)
    return jnp.concatenate([mul(bar_first, inverse_first), bar_updated], axis=1)
```

```python
import jax
import jax.numpy as jnp
from jax import lax
from jax.experimental import pallas as pl
from jax.experimental.pallas import tpu as pltpu
from jax.sharding import PartitionSpec as P

MESH = pl.DeviceIdType.MESH
NX, NY, NZ, NC = 4, 8, 8, 2
ROWS, COLS, STRIP, PANEL = 1280, 640, 128, 64
PART = ROWS // NX
SUB = PART // NY
PIECE = COLS // NX // NC
Y_FAR = (4, 3, 5, 2, 6, 1, 7)
Y_NEAR = (1, 7, 2, 6, 3, 5, 4)
X_FAR = (2, 1, 3)
Z_FAR = (4, 3, 5, 2, 6, 1, 7)
C_CHUNKS = 5


def exact(left, right, dims=((1,), (0,))):
    return lax.dot_general(
        left, right, (dims, ((), ())),
        precision=lax.Precision.HIGHEST, preferred_element_type=jnp.float32,
    )


def halves(value):
    high = value.astype(jnp.bfloat16)
    low = (value - high.astype(jnp.float32)).astype(jnp.bfloat16)
    return high, low


def rows_of(start, size):
    return pl.ds(pl.multiple_of(start, 8), size)


def kernel(
    strip_h, below_h, first_h, second_h, cot_h, out_h,
    strip_v, below_v, first_v, second_v, cot_v, split_v, lower_v, column_v, relay_v,
    weights_v, back_v, backs_v, backsum_v, backin_v,
    part_v, xin_v, ysend_v, yin_v, out_v, unit_v,
    load_sem, store_sem, peer_sem,
    s1, r1, s2, r2, s3, r3, sb, rb, sf, rf, sx, rx, sy, ry, syg, ryg, sxg, rxg,
):
    row, col = lax.axis_index("row"), lax.axis_index("col")
    z, c = row // NC, row % NC
    x, y = col // NY, col % NY

    def at(z_, c_, x_, y_):
        return (z_ * NC + c_, x_ * NY + y_)

    def send(src, dst, ssem, rsem, device):
        copy = pltpu.make_async_remote_copy(
            src_ref=src, dst_ref=dst, send_sem=ssem, recv_sem=rsem,
            device_id=device, device_id_type=MESH,
        )
        copy.start()
        return copy

    def arrived(dst, rsem):
        pltpu.make_async_copy(dst, dst, rsem).wait()

    def turn(base, d, n):
        return lax.rem(base + d, n)

    barrier = pltpu.get_barrier_semaphore()
    peers = []
    for d in range(1, NX):
        peers += [at(z, c, turn(x, d, NX), y), at(z, 1 - c, turn(x, d, NX), y)]
    for d in range(1, NY):
        peers.append(at(z, c, x, turn(y, d, NY)))
    for d in range(1, NZ):
        peers += [at(turn(z, d, NZ), c, x, y), at(turn(z, d, NZ), 1 - c, x, y)]
    peers.append(at(z, 1 - c, x, y))
    for peer in peers:
        pl.semaphore_signal(barrier, inc=1, device_id=peer, device_id_type=MESH)

    small = []
    for i, (src, dst) in enumerate(((below_h, below_v), (first_h, first_v), (second_h, second_v), (strip_h, strip_v))):
        copy = pltpu.make_async_copy(src, dst, load_sem.at[i])
        copy.start()
        small.append(copy)
    chunk = ROWS // C_CHUNKS
    loads = []
    for i in range(C_CHUNKS):
        rows = pl.ds(i * chunk, chunk)
        copy = pltpu.make_async_copy(cot_h.at[rows], cot_v.at[rows], load_sem.at[4 + i])
        copy.start()
        loads.append(copy)

    for copy in small[:3]:
        copy.wait()
    first, second = first_v[...], second_v[...]
    left = exact(below_v[...], first, ((1,), (1,)))
    mixed = exact(exact(second, left), first)
    unit_v[0:PANEL, 0:PANEL] = first
    unit_v[0:PANEL, PANEL:] = jnp.zeros_like(first)
    unit_v[PANEL:, 0:PANEL] = -mixed
    unit_v[PANEL:, PANEL:] = second
    small[3].wait()
    lower_v[...] = exact(strip_v[...], unit_v[...], ((1,), (1,)))

    pl.semaphore_wait(barrier, len(peers))
    for d in range(1, NX):
        pl.semaphore_signal(peer_sem, inc=1, device_id=at(z, c, turn(x, d, NX), y), device_id_type=MESH)

    is_source = (y // 2) == lax.rem(row, NX)
    target_x = row // NX
    source_rows = lax.rem(y, 2) * COLS
    in_plane = (2 * x + y // NX) == z
    has_block = jnp.logical_and(in_plane, lax.rem(y // 2, NC) == c)

    @pl.when(is_source)
    def _():
        for i, d in enumerate(Z_FAR):
            for h in range(NC):
                src = lower_v.at[rows_of(source_rows + (x * NC + h) * PIECE, PIECE)]
                send(src, relay_v.at[target_x], s1.at[i * NC + h], r1.at[target_x], at(turn(z, d, NZ), h, x, y))

    @pl.when(has_block)
    def _():
        send(lower_v.at[rows_of(source_rows, COLS)], column_v, s3.at[0], r3.at[0], at(z, 1 - c, x, y))
        column_v[...] = lower_v[rows_of(source_rows, COLS), :]

    for i in range(C_CHUNKS):
        loads[i].wait()
        rows = pl.ds(i * chunk, chunk)
        high, low = halves(cot_v[rows, :])
        split_v[rows, 0:COLS] = high
        split_v[rows, COLS:] = low

    high, low = halves(jnp.transpose(lower_v[...]))
    back = jnp.dot(jnp.concatenate([high, low], axis=0), split_v[...], preferred_element_type=jnp.float32)
    back = back[0:STRIP] + back[STRIP:]
    back_v[...] = jnp.transpose(back[:, 0:COLS] + back[:, COLS:])
    pl.semaphore_wait(peer_sem, NX - 1)
    mine = z * NC + (1 - c)
    for d in (4, 3, 5, 2, 6, 1, 7, 0):
        for e in range(NC):
            if d == 0 and e == 0:
                continue
            z_, c_ = turn(z, d, NZ), lax.rem(c + e, NC)
            src = back_v.at[rows_of((z_ * NC + 1 - c_) * SUB, SUB)]
            k = d * NC + e
            send(src, backs_v.at[k], sb.at[k], rb.at[k], at(z_, c_, x, y))

    for d in (1, 3, 2, 0):
        x_ = turn(x, d, NX)

        @pl.when((2 * x_ + y // NX) != z)
        def _(d=d, x_=x_):
            arrived(relay_v.at[x_], r1.at[x_])
            here = rows_of((x * NC + c) * PIECE, PIECE)
            for e in range(NC):
                if d == 0 and e == 0:
                    column_v[here, :] = relay_v[x_]
                    continue
                k = d * NC + e
                send(relay_v.at[x_], column_v.at[here], s2.at[k], r2.at[x * NC + c], at(z, lax.rem(c + e, NC), x_, y))

    @pl.when(jnp.logical_not(in_plane))
    def _():
        for d in range(NX):
            for e in range(NC):
                if d == 0 and e == 0:
                    continue
                k = turn(x, d, NX) * NC + lax.rem(c + e, NC)
                arrived(column_v.at[rows_of(k * PIECE, PIECE)], r2.at[k])

    @pl.when(jnp.logical_and(in_plane, jnp.logical_not(has_block)))
    def _():
        arrived(column_v, r3.at[0])

    high, low = halves(column_v[...])
    both = jnp.concatenate([high, low], axis=1)
    weights_v[0:COLS, :] = both
    weights_v[COLS:, :] = both
    for d in X_FAR + (0,):
        x_ = turn(x, d, NX)
        part = jnp.dot(
            split_v[pl.ds(pl.multiple_of(x_ * PART, 16), PART), :], weights_v[...],
            preferred_element_type=jnp.float32,
        )
        part_v[rows_of(x_ * PART, PART), :] = part[:, 0:STRIP] + part[:, STRIP:]
        if d:
            for e in Y_FAR + (0,):
                y_ = turn(y, e, NY)
                src = part_v.at[rows_of(x_ * PART + y_ * SUB, SUB)]
                k = (d - 1) * NY + e
                send(src, xin_v.at[d - 1, e], sx.at[k], rx.at[k], at(z, c, x_, y))

    total = back_v[rows_of(mine * SUB, SUB), :]
    for k in range(1, NZ * NC):
        arrived(backs_v.at[k], rb.at[k])
        total = total + backs_v[k]
    backsum_v[...] = total
    send(backsum_v, backin_v, sf.at[0], rf.at[0], (col // 2, lax.rem(col, 2) * (NZ * NC) + mine))

    kept = None
    for e in Y_FAR + (0,):
        y_ = turn(y, e, NY)
        total = part_v[rows_of(x * PART + y_ * SUB, SUB), :]
        for d in range(1, NX):
            k = (d - 1) * NY + e
            arrived(xin_v.at[d - 1, e], rx.at[k])
            total = total + xin_v[d - 1, e]
        if e:
            ysend_v[e] = total
            send(ysend_v.at[e], yin_v.at[e], sy.at[e], ry.at[e], at(z, c, x, y_))
        else:
            kept = total
    for e in range(1, NY):
        arrived(yin_v.at[e], ry.at[e])
        kept = kept + yin_v[e]
    arrived(backin_v, rf.at[0])
    kept = kept + backin_v[...]

    here = rows_of(x * PART + y * SUB, SUB)
    out_v[here, :] = -exact(kept, unit_v[...])
    for e in Y_FAR:
        send(out_v.at[here], out_v.at[here], syg.at[e], ryg.at[e], at(z, c, x, turn(y, e, NY)))

    for e in (0,) + Y_NEAR:
        y_ = turn(y, NY - e, NY)
        block = out_v.at[rows_of(x * PART + y_ * SUB, SUB)]
        if e:
            arrived(block, ryg.at[e])
        for d in X_FAR:
            k = (d - 1) * NY + e
            send(block, block, sxg.at[k], rxg.at[k], at(z, c, turn(x, d, NX), y))

    stores = []
    for d in (0, 1, 3, 2):
        x_ = turn(x, NX - d, NX)
        rows = rows_of(x_ * PART, PART)
        if d:
            for e in range(NY):
                y_ = turn(y, NY - e, NY)
                arrived(out_v.at[rows_of(x_ * PART + y_ * SUB, SUB)], rxg.at[(d - 1) * NY + e])
        copy = pltpu.make_async_copy(out_v.at[rows], out_h.at[rows], store_sem.at[d])
        copy.start()
        stores.append(copy)

    def left_here(ref, sem):
        pltpu.make_async_copy(ref, ref, sem).wait()

    @pl.when(is_source)
    def _():
        for i in range((NZ - 1) * NC):
            left_here(relay_v.at[0], s1.at[i])

    @pl.when(has_block)
    def _():
        left_here(column_v, s3.at[0])

    for d in range(NX):
        x_ = turn(x, d, NX)

        @pl.when((2 * x_ + y // NX) != z)
        def _(d=d):
            for e in range(NC):
                if d or e:
                    left_here(relay_v.at[0], s2.at[d * NC + e])

    for k in range(1, NZ * NC):
        left_here(backs_v.at[k], sb.at[k])
    left_here(backsum_v, sf.at[0])
    for k in range((NX - 1) * NY):
        left_here(backsum_v, sx.at[k])
        left_here(backsum_v, sxg.at[k])
    for e in range(1, NY):
        left_here(backsum_v, sy.at[e])
        left_here(backsum_v, syg.at[e])
    for copy in stores:
        copy.wait()


def shards(strip, below, first, second, cotangent):
    f32, bf16 = jnp.float32, jnp.bfloat16
    dma = pltpu.SemaphoreType.DMA
    pairs = (
        (NZ - 1) * NC, NX, NX * NC, NX * NC, 1, 1, NZ * NC, NZ * NC, 1, 1,
        (NX - 1) * NY, (NX - 1) * NY, NY, NY, NY, NY, (NX - 1) * NY, (NX - 1) * NY,
    )
    return pl.pallas_call(
        kernel,
        out_shape=jax.ShapeDtypeStruct((ROWS, STRIP), f32),
        in_specs=[pl.BlockSpec(memory_space=pl.ANY)] * 5,
        out_specs=pl.BlockSpec(memory_space=pl.ANY),
        scratch_shapes=[
            pltpu.VMEM((ROWS, STRIP), f32),
            pltpu.VMEM((PANEL, PANEL), f32),
            pltpu.VMEM((PANEL, PANEL), f32),
            pltpu.VMEM((PANEL, PANEL), f32),
            pltpu.VMEM((ROWS, COLS), f32),
            pltpu.VMEM((ROWS, 2 * COLS), bf16),
            pltpu.VMEM((ROWS, STRIP), f32),
            pltpu.VMEM((COLS, STRIP), f32),
            pltpu.VMEM((NX, PIECE, STRIP), f32),
            pltpu.VMEM((2 * COLS, 2 * STRIP), bf16),
            pltpu.VMEM((COLS, STRIP), f32),
            pltpu.VMEM((NZ * NC, SUB, STRIP), f32),
            pltpu.VMEM((SUB, STRIP), f32),
            pltpu.VMEM((SUB, STRIP), f32),
            pltpu.VMEM((ROWS, STRIP), f32),
            pltpu.VMEM((NX - 1, NY, SUB, STRIP), f32),
            pltpu.VMEM((NY, SUB, STRIP), f32),
            pltpu.VMEM((NY, SUB, STRIP), f32),
            pltpu.VMEM((ROWS, STRIP), f32),
            pltpu.VMEM((STRIP, STRIP), f32),
            dma((4 + C_CHUNKS,)),
            dma((NX,)),
            pltpu.SemaphoreType.REGULAR,
        ] + [dma((n,)) for n in pairs],
        compiler_params=pltpu.CompilerParams(
            collective_id=0, has_side_effects=True, vmem_limit_bytes=40 << 20,
        ),
    )(strip, below, first, second, cotangent)


def solution(mesh):
    return jax.shard_map(
        shards,
        mesh=mesh,
        in_specs=(P("row", None), P(), P(), P(), P("row", "col")),
        out_specs=P("row", None),
        check_vma=False,
    )
```

```python
import jax
import jax.numpy as jnp
from jax import lax
from jax.experimental import pallas as pl
from jax.experimental.pallas import tpu as pltpu
from jax.sharding import PartitionSpec as P

MESH = pl.DeviceIdType.MESH
NX, NY, NZ, NC = 4, 8, 8, 2
ROWS, COLS, STRIP, PANEL = 1280, 640, 128, 64
HALF = ROWS // 2
MAIN, REST = 32, 8
SUB = MAIN + REST
PART = MAIN * NY
EDGE = PART * 2
PIECE = COLS // NX // NC
Y_FAR = (4, 3, 5, 2, 6, 1, 7)
Y_NEAR = (1, 7, 2, 6, 3, 5, 4)
X_FAR = (2, 1, 3)
Z_FAR = (4, 3, 5, 2, 6, 1, 7)
C_CHUNKS = 5


def exact(left, right, dims=((1,), (0,))):
    return lax.dot_general(
        left, right, (dims, ((), ())),
        precision=lax.Precision.HIGHEST, preferred_element_type=jnp.float32,
    )


def halves(value):
    high = value.astype(jnp.bfloat16)
    low = (value - high.astype(jnp.float32)).astype(jnp.bfloat16)
    return high, low


def rows_of(start, size):
    return pl.ds(pl.multiple_of(start, 8), size)


def kernel(
    strip_h, below_h, first_h, second_h, cot_h, out_v,
    strip_v, below_v, first_v, second_v, cot_v, split_v, column_v, relay_v, weights_v,
    back_v, pairin_v, backs_v, backsum_v, backin_v,
    part_v, xin_v, ysend_v, yin_v, yin2_v, xsend2_v, xin2_v, unit_v,
    load_sem, peer_sem,
    s1, r1, s2, r2, s3, r3, sp, rp, sb, rb, sf, rf, sx, rx, sy, ry, syg, ryg, sxg, rxg,
    sy2, ry2, sx2, rx2, sxg2, rxg2, syg2, ryg2,
):
    row, col = lax.axis_index("row"), lax.axis_index("col")
    z, c = row // NC, row % NC
    x, y = col // NY, col % NY

    def at(z_, c_, x_, y_):
        return (z_ * NC + c_, x_ * NY + y_)

    def send(src, dst, ssem, rsem, device):
        copy = pltpu.make_async_remote_copy(
            src_ref=src, dst_ref=dst, send_sem=ssem, recv_sem=rsem,
            device_id=device, device_id_type=MESH,
        )
        copy.start()
        return copy

    def arrived(dst, rsem):
        pltpu.make_async_copy(dst, dst, rsem).wait()

    def turn(base, d, n):
        return lax.rem(base + d, n)

    barrier = pltpu.get_barrier_semaphore()
    peers = []
    for d in range(1, NX):
        peers += [at(z, c, turn(x, d, NX), y), at(z, 1 - c, turn(x, d, NX), y)]
    for d in range(1, NY):
        peers.append(at(z, c, x, turn(y, d, NY)))
    for d in range(1, NZ):
        peers += [at(turn(z, d, NZ), c, x, y), at(turn(z, d, NZ), 1 - c, x, y)]
    peers.append(at(z, 1 - c, x, y))
    for peer in peers:
        pl.semaphore_signal(barrier, inc=1, device_id=peer, device_id_type=MESH)

    small = []
    for i, (src, dst) in enumerate(((below_h, below_v), (first_h, first_v), (second_h, second_v), (strip_h, strip_v))):
        copy = pltpu.make_async_copy(src, dst, load_sem.at[i])
        copy.start()
        small.append(copy)
    chunk = ROWS // C_CHUNKS
    loads = []
    for i in range(C_CHUNKS):
        rows = pl.ds(i * chunk, chunk)
        copy = pltpu.make_async_copy(cot_h.at[rows], cot_v.at[rows], load_sem.at[4 + i])
        copy.start()
        loads.append(copy)

    pl.semaphore_wait(barrier, len(peers))
    for d in range(1, NX):
        pl.semaphore_signal(peer_sem, inc=1, device_id=at(z, c, turn(x, d, NX), y), device_id_type=MESH)

    is_source = (y // 2) == lax.rem(row, 4)
    target_x = row // 4
    source_rows = lax.rem(y, 2) * COLS
    in_plane = (2 * x + y // 4) == z
    has_block = jnp.logical_and(in_plane, lax.rem(y // 2, NC) == c)

    @pl.when(is_source)
    def _():
        for i, d in enumerate(Z_FAR):
            for h in range(NC):
                src = strip_h.at[rows_of(source_rows + (x * NC + h) * PIECE, PIECE)]
                send(src, relay_v.at[target_x], s1.at[i * NC + h], r1.at[target_x], at(turn(z, d, NZ), h, x, y))

    @pl.when(has_block)
    def _():
        send(strip_h.at[rows_of(source_rows, COLS)], column_v, s3.at[0], r3.at[0], at(z, 1 - c, x, y))

    for copy in small[:3]:
        copy.wait()
    first, second = first_v[...], second_v[...]
    left = exact(below_v[...], first, ((1,), (1,)))
    mixed = exact(exact(second, left), first)
    unit_v[0:PANEL, 0:PANEL] = first
    unit_v[0:PANEL, PANEL:] = jnp.zeros_like(first)
    unit_v[PANEL:, 0:PANEL] = -mixed
    unit_v[PANEL:, PANEL:] = second
    small[3].wait()

    for i in range(C_CHUNKS):
        loads[i].wait()
        rows = pl.ds(i * chunk, chunk)
        high, low = halves(cot_v[rows, :])
        split_v[rows, 0:COLS] = high
        split_v[rows, COLS:] = low

    high, low = halves(jnp.transpose(exact(strip_v[...], unit_v[...], ((1,), (1,)))))
    back = jnp.dot(jnp.concatenate([high, low], axis=0), split_v[...], preferred_element_type=jnp.float32)
    back = back[0:STRIP] + back[STRIP:]
    back = jnp.transpose(back[:, 0:COLS] + back[:, COLS:])
    pieces = NZ * NC
    for k in range(pieces):
        back_v[1 - k % 2, k // 2, 0:MAIN] = back[k * MAIN:(k + 1) * MAIN]
        rest = pieces * MAIN + (k % NY * 2 + k // NY) * REST
        back_v[1 - k % 2, k // 2, MAIN:] = back[rest:rest + REST]
    pl.semaphore_wait(peer_sem, NX - 1)
    send(back_v.at[1 - c], pairin_v, sp.at[0], rp.at[0], at(z, 1 - c, x, y))

    for d in (1, 3, 2, 0):
        x_ = turn(x, d, NX)

        @pl.when((2 * x_ + y // 4) != z)
        def _(d=d, x_=x_):
            arrived(relay_v.at[x_], r1.at[x_])
            here = rows_of((x * NC + c) * PIECE, PIECE)
            for e in range(NC):
                if d == 0 and e == 0:
                    column_v[here, :] = relay_v[x_]
                    continue
                k = d * NC + e
                send(relay_v.at[x_], column_v.at[here], s2.at[k], r2.at[x * NC + c], at(z, lax.rem(c + e, NC), x_, y))

    arrived(pairin_v, rp.at[0])
    back_v[c] = back_v[c] + pairin_v[...]
    for d in Z_FAR:
        z_ = turn(z, d, NZ)
        send(back_v.at[c, z_], backs_v.at[d], sb.at[d], rb.at[d], at(z_, c, x, y))

    @pl.when(has_block)
    def _():
        column_v[...] = strip_v[rows_of(source_rows, COLS), :]

    @pl.when(jnp.logical_and(in_plane, jnp.logical_not(has_block)))
    def _():
        arrived(column_v, r3.at[0])

    for d in (0, 1, 3, 2):
        x_ = turn(x, d, NX)

        @pl.when(jnp.logical_not(in_plane))
        def _(d=d, x_=x_):
            for e in range(NC):
                if d or e:
                    k = x_ * NC + lax.rem(c + e, NC)
                    arrived(column_v.at[rows_of(k * PIECE, PIECE)], r2.at[k])

        start, size = x_ * (NC * PIECE), NC * PIECE
        high, low = halves(exact(column_v[rows_of(start, size), :], unit_v[...], ((1,), (1,))))
        both = jnp.concatenate([high, low], axis=1)
        weights_v[pl.ds(pl.multiple_of(start, 32), size), :] = both
        weights_v[pl.ds(pl.multiple_of(COLS + start, 32), size), :] = both

    def product(start, size):
        part = jnp.dot(
            split_v[pl.ds(pl.multiple_of(start, 128), size), :], weights_v[...],
            preferred_element_type=jnp.float32,
        )
        return part[:, 0:STRIP] + part[:, STRIP:]

    for half in range(2):
        part_v[half, EDGE:HALF] = product(half * HALF + EDGE, HALF - EDGE)
    for e in Y_FAR:
        y_ = turn(y, e, NY)
        send(part_v.at[:, rows_of(EDGE + y_ * 2 * REST, 2 * REST)], yin2_v.at[e], sy2.at[e], ry2.at[e], at(z, c, x, y_))
    for d in X_FAR + (0,):
        x_ = turn(x, d, NX)
        half, start = x_ // 2, lax.rem(x_, 2) * PART
        part_v[half, rows_of(start, PART), :] = product(half * HALF + start, PART)
        if d:
            for e in Y_FAR + (0,):
                y_ = turn(y, e, NY)
                k = (d - 1) * NY + e
                send(part_v.at[half, rows_of(start + y_ * MAIN, MAIN)], xin_v.at[d - 1, e], sx.at[k], rx.at[k], at(z, c, x_, y))

    mine, low_x = x // 2, lax.rem(x, 2)
    kept = None
    for i, e in enumerate(Y_FAR + (0,)):
        if i == 3:
            total = back_v[c, z]
            for d in range(1, NZ):
                arrived(backs_v.at[d], rb.at[d])
                total = total + backs_v[d]
            backsum_v[...] = total
            target = lax.rem(col, 2) * pieces + z * NC + (1 - c)
            send(backsum_v, backin_v, sf.at[0], rf.at[0], (col // 2, target))
        if i == 6:
            total = part_v[:, rows_of(EDGE + y * 2 * REST, 2 * REST), :]
            for d in range(1, NY):
                arrived(yin2_v.at[d], ry2.at[d])
                total = total + yin2_v[d]
            xsend2_v[...] = total
            for d in X_FAR:
                x_ = turn(x, d, NX)
                src = xsend2_v.at[x_ // 2, rows_of(lax.rem(x_, 2) * REST, REST)]
                send(src, xin2_v.at[d], sx2.at[d], rx2.at[d], at(z, c, x_, y))
        y_ = turn(y, e, NY)
        total = part_v[mine, rows_of(low_x * PART + y_ * MAIN, MAIN), :]
        for d in range(1, NX):
            k = (d - 1) * NY + e
            arrived(xin_v.at[d - 1, e], rx.at[k])
            total = total + xin_v[d - 1, e]
        if e:
            ysend_v[e] = total
            send(ysend_v.at[e], yin_v.at[e], sy.at[e], ry.at[e], at(z, c, x, y_))
        else:
            kept = total
    rest = xsend2_v[mine, rows_of(low_x * REST, REST), :]
    for d in range(1, NX):
        arrived(xin2_v.at[d], rx2.at[d])
        rest = rest + xin2_v[d]
    for e in range(1, NY):
        arrived(yin_v.at[e], ry.at[e])
        kept = kept + yin_v[e]
    kept = jnp.concatenate([kept, rest], axis=0)
    arrived(backin_v, rf.at[0])
    done = -exact(kept + backin_v[...], unit_v[...])

    def main_rows(x_, y_):
        return out_v.at[x_ // 2, rows_of(lax.rem(x_, 2) * PART + y_ * MAIN, MAIN)]

    def rest_rows(x_, y_):
        return out_v.at[x_ // 2, rows_of(EDGE + y_ * 2 * REST + lax.rem(x_, 2) * REST, REST)]

    def rest_part(y_):
        return out_v.at[:, rows_of(EDGE + y_ * 2 * REST, 2 * REST)]

    main_rows(x, y)[...] = done[0:MAIN]
    rest_rows(x, y)[...] = done[MAIN:]
    for d in X_FAR:
        send(rest_rows(x, y), rest_rows(x, y), sxg2.at[d], rxg2.at[d], at(z, c, turn(x, d, NX), y))
    for e in Y_FAR:
        send(main_rows(x, y), main_rows(x, y), syg.at[e], ryg.at[e], at(z, c, x, turn(y, e, NY)))

    for e in (0,) + Y_NEAR:
        block = main_rows(x, turn(y, NY - e, NY))
        if e:
            arrived(block, ryg.at[e])
        for d in X_FAR:
            k = (d - 1) * NY + e
            send(block, block, sxg.at[k], rxg.at[k], at(z, c, turn(x, d, NX), y))
        if e == 1:
            for d in range(1, NX):
                arrived(rest_rows(turn(x, NX - d, NX), y), rxg2.at[d])
            for d in Y_FAR:
                send(rest_part(y), rest_part(y), syg2.at[d], ryg2.at[d], at(z, c, x, turn(y, d, NY)))

    for d in range(1, NX):
        for e in range(NY):
            arrived(main_rows(turn(x, NX - d, NX), turn(y, NY - e, NY)), rxg.at[(d - 1) * NY + e])
    for e in range(1, NY):
        arrived(rest_part(turn(y, NY - e, NY)), ryg2.at[e])

    def left_here(ref, sem):
        pltpu.make_async_copy(ref, ref, sem).wait()

    @pl.when(is_source)
    def _():
        for i in range((NZ - 1) * NC):
            left_here(relay_v.at[0], s1.at[i])

    @pl.when(has_block)
    def _():
        left_here(column_v, s3.at[0])

    for d in range(NX):
        x_ = turn(x, d, NX)

        @pl.when((2 * x_ + y // 4) != z)
        def _(d=d):
            for e in range(NC):
                if d or e:
                    left_here(relay_v.at[0], s2.at[d * NC + e])

    left_here(pairin_v, sp.at[0])
    for d in range(1, NZ):
        left_here(backs_v.at[d], sb.at[d])
    left_here(backsum_v, sf.at[0])
    for k in range((NX - 1) * NY):
        left_here(xin_v.at[0, 0], sx.at[k])
        left_here(xin_v.at[0, 0], sxg.at[k])
    for e in range(1, NY):
        left_here(yin_v.at[e], sy.at[e])
        left_here(yin_v.at[e], syg.at[e])
        left_here(yin2_v.at[e], sy2.at[e])
        left_here(yin2_v.at[e], syg2.at[e])
    for d in range(1, NX):
        left_here(xin2_v.at[d], sx2.at[d])
        left_here(xin2_v.at[d], sxg2.at[d])


def shards(strip, below, first, second, cotangent):
    f32, bf16 = jnp.float32, jnp.bfloat16
    dma = pltpu.SemaphoreType.DMA
    main = (NX - 1) * NY
    pairs = (
        (NZ - 1) * NC, NX, NX * NC, NX * NC, 1, 1, 1, 1, NZ, NZ, 1, 1,
        main, main, NY, NY, NY, NY, main, main,
        NY, NY, NX, NX, NX, NX, NY, NY,
    )
    out = pl.pallas_call(
        kernel,
        out_shape=pltpu.VMEM((2, HALF, STRIP), f32),
        in_specs=[pl.BlockSpec(memory_space=pltpu.HBM)] * 5,
        out_specs=pl.BlockSpec(memory_space=pltpu.VMEM),
        scratch_shapes=[
            pltpu.VMEM((ROWS, STRIP), f32),
            pltpu.VMEM((PANEL, PANEL), f32),
            pltpu.VMEM((PANEL, PANEL), f32),
            pltpu.VMEM((PANEL, PANEL), f32),
            pltpu.VMEM((ROWS, COLS), f32),
            pltpu.VMEM((ROWS, 2 * COLS), bf16),
            pltpu.VMEM((COLS, STRIP), f32),
            pltpu.VMEM((NX, PIECE, STRIP), f32),
            pltpu.VMEM((2 * COLS, 2 * STRIP), bf16),
            pltpu.VMEM((NC, NZ, SUB, STRIP), f32),
            pltpu.VMEM((NZ, SUB, STRIP), f32),
            pltpu.VMEM((NZ, SUB, STRIP), f32),
            pltpu.VMEM((SUB, STRIP), f32),
            pltpu.VMEM((SUB, STRIP), f32),
            pltpu.VMEM((2, HALF, STRIP), f32),
            pltpu.VMEM((NX - 1, NY, MAIN, STRIP), f32),
            pltpu.VMEM((NY, MAIN, STRIP), f32),
            pltpu.VMEM((NY, MAIN, STRIP), f32),
            pltpu.VMEM((NY, 2, 2 * REST, STRIP), f32),
            pltpu.VMEM((2, 2 * REST, STRIP), f32),
            pltpu.VMEM((NX, REST, STRIP), f32),
            pltpu.VMEM((STRIP, STRIP), f32),
            dma((4 + C_CHUNKS,)),
            pltpu.SemaphoreType.REGULAR,
        ] + [dma((n,)) for n in pairs],
        compiler_params=pltpu.CompilerParams(
            collective_id=0, has_side_effects=True, vmem_limit_bytes=40 << 20,
        ),
    )(*[pltpu.with_memory_space_constraint(v, pltpu.HBM) for v in (strip, below, first, second, cotangent)])
    return out.reshape(ROWS, STRIP)


def solution(mesh):
    return jax.shard_map(
        shards,
        mesh=mesh,
        in_specs=(P("row", None), P(), P(), P(), P("row", "col")),
        out_specs=P("row", None),
        check_vma=False,
    )
```

```python
import jax
import jax.numpy as jnp
from jax import lax
from jax.experimental import pallas as pl
from jax.experimental.pallas import tpu as pltpu
from jax.sharding import PartitionSpec as P

MESH = pl.DeviceIdType.MESH
NX, NY, NZ, NC = 4, 8, 8, 2
ROWS, COLS, STRIP, PANEL = 1280, 640, 128, 64
HALF = ROWS // 2
MAIN, REST = 32, 8
SUB = MAIN + REST
PART = MAIN * NY
EDGE = PART * 2
PIECE = COLS // NX // NC
Y_FAR = (4, 3, 5, 2, 6, 1, 7)
Y_NEAR = (1, 7, 2, 6, 3, 5, 4)
X_FAR = (2, 1, 3)
Z_FAR = (4, 3, 5, 2, 6, 1, 7)
C_CHUNKS = 5


def exact(left, right, dims=((1,), (0,))):
    return lax.dot_general(
        left, right, (dims, ((), ())),
        precision=lax.Precision.HIGHEST, preferred_element_type=jnp.float32,
    )


def halves(value):
    high = value.astype(jnp.bfloat16)
    low = (value - high.astype(jnp.float32)).astype(jnp.bfloat16)
    return high, low


def rows_of(start, size):
    return pl.ds(pl.multiple_of(start, 8), size)


def kernel(
    strip_h, below_h, first_h, second_h, cot_h, out_v,
    strip_v, below_v, first_v, second_v, cot_v, split_v, column_v, weights_v,
    back_v, pairin_v, backs_v, backsum_v, backin_v,
    part_v, xin_v, ysend_v, yin_v, yin2_v, xsend2_v, xin2_v, unit_v,
    load_sem, peer_sem,
    s1, r1, s2, r2, s3, r3, sp, rp, sb, rb, sf, rf, sx, rx, sy, ry, syg, ryg, sxg, rxg,
    sy2, ry2, sx2, rx2, sxg2, rxg2, syg2, ryg2,
):
    row, col = lax.axis_index("row"), lax.axis_index("col")
    z, c = row // NC, row % NC
    x, y = col // NY, col % NY

    def at(z_, c_, x_, y_):
        return (z_ * NC + c_, x_ * NY + y_)

    def send(src, dst, ssem, rsem, device):
        copy = pltpu.make_async_remote_copy(
            src_ref=src, dst_ref=dst, send_sem=ssem, recv_sem=rsem,
            device_id=device, device_id_type=MESH,
        )
        copy.start()
        return copy

    def arrived(dst, rsem):
        pltpu.make_async_copy(dst, dst, rsem).wait()

    def turn(base, d, n):
        return lax.rem(base + d, n)

    is_source = (y // 2) == lax.rem(row, 4)
    target_x = row // 4
    source_rows = lax.rem(y, 2) * COLS
    in_plane = (2 * x + y // 4) == z
    has_block = jnp.logical_and(in_plane, lax.rem(y // 2, NC) == c)

    barrier = pltpu.get_barrier_semaphore()

    def greet(peer):
        pl.semaphore_signal(barrier, inc=1, device_id=peer, device_id_type=MESH)

    @pl.when(jnp.logical_not(in_plane))
    def _():
        for x_ in range(NX):
            greet(at(2 * x + y // 4, lax.rem(y // 2, NC), x_, y))

    peers = [at(z, 1 - c, x, y)]
    peers += [at(turn(z, d, NZ), c, x, y) for d in Z_FAR]
    peers += [at(z, c, x, turn(y, d, NY)) for d in Y_FAR]
    peers += [at(z, c, turn(x, d, NX), y) for d in X_FAR]
    for peer in peers:
        greet(peer)

    small = []
    for i, (src, dst) in enumerate(((below_h, below_v), (first_h, first_v), (second_h, second_v), (strip_h, strip_v))):
        copy = pltpu.make_async_copy(src, dst, load_sem.at[i])
        copy.start()
        small.append(copy)
    chunk = ROWS // C_CHUNKS
    loads = []
    for i in range(C_CHUNKS):
        rows = pl.ds(i * chunk, chunk)
        copy = pltpu.make_async_copy(cot_h.at[rows], cot_v.at[rows], load_sem.at[4 + i])
        copy.start()
        loads.append(copy)

    pl.semaphore_wait(barrier, len(peers) + jnp.where(is_source, (NZ - 1) * NC, 0))
    for d in range(1, NX):
        pl.semaphore_signal(peer_sem, inc=1, device_id=at(z, c, turn(x, d, NX), y), device_id_type=MESH)

    @pl.when(is_source)
    def _():
        for i, d in enumerate(Z_FAR):
            for h in range(NC):
                src = strip_h.at[rows_of(source_rows + (x * NC + h) * PIECE, PIECE)]
                dst = column_v.at[rows_of((x * NC + h) * PIECE, PIECE)]
                send(src, dst, s1.at[i * NC + h], r1.at[x], at(turn(z, d, NZ), h, target_x, y))

    @pl.when(has_block)
    def _():
        send(strip_h.at[rows_of(source_rows, COLS)], column_v, s3.at[0], r3.at[0], at(z, 1 - c, x, y))

    for copy in small[:3]:
        copy.wait()
    first, second = first_v[...], second_v[...]
    left = exact(below_v[...], first, ((1,), (1,)))
    mixed = exact(exact(second, left), first)
    unit_v[0:PANEL, 0:PANEL] = first
    unit_v[0:PANEL, PANEL:] = jnp.zeros_like(first)
    unit_v[PANEL:, 0:PANEL] = -mixed
    unit_v[PANEL:, PANEL:] = second
    small[3].wait()

    for i in range(C_CHUNKS):
        loads[i].wait()
        rows = pl.ds(i * chunk, chunk)
        high, low = halves(cot_v[rows, :])
        split_v[rows, 0:COLS] = high
        split_v[rows, COLS:] = low

    high, low = halves(jnp.transpose(exact(strip_v[...], unit_v[...], ((1,), (1,)))))
    back = jnp.dot(jnp.concatenate([high, low], axis=0), split_v[...], preferred_element_type=jnp.float32)
    back = back[0:STRIP] + back[STRIP:]
    back = jnp.transpose(back[:, 0:COLS] + back[:, COLS:])
    pieces = NZ * NC
    for k in range(pieces):
        back_v[1 - k % 2, k // 2, 0:MAIN] = back[k * MAIN:(k + 1) * MAIN]
        rest = pieces * MAIN + (k % NY * 2 + k // NY) * REST
        back_v[1 - k % 2, k // 2, MAIN:] = back[rest:rest + REST]
    pl.semaphore_wait(peer_sem, NX - 1)
    send(back_v.at[1 - c], pairin_v, sp.at[0], rp.at[0], at(z, 1 - c, x, y))

    arrived(pairin_v, rp.at[0])
    back_v[c] = back_v[c] + pairin_v[...]
    for d in Z_FAR:
        z_ = turn(z, d, NZ)
        send(back_v.at[c, z_], backs_v.at[d], sb.at[d], rb.at[d], at(z_, c, x, y))

    @pl.when(has_block)
    def _():
        column_v[...] = strip_v[rows_of(source_rows, COLS), :]

    @pl.when(jnp.logical_and(in_plane, jnp.logical_not(has_block)))
    def _():
        arrived(column_v, r3.at[0])

    def lower_of(k):
        start = k * PIECE
        high, low = halves(exact(column_v[rows_of(start, PIECE), :], unit_v[...], ((1,), (1,))))
        both = jnp.concatenate([high, low], axis=1)
        weights_v[pl.ds(pl.multiple_of(start, 16), PIECE), :] = both
        weights_v[pl.ds(pl.multiple_of(COLS + start, 16), PIECE), :] = both

    for d in (0, 1, 3, 2):
        x_ = turn(x, d, NX)
        k = x_ * NC + c

        @pl.when(jnp.logical_not(in_plane))
        def _(d=d, x_=x_, k=k):
            block = column_v.at[rows_of(k * PIECE, PIECE)]
            arrived(block, r1.at[x_])
            send(block, block, s2.at[d], r2.at[x_], at(z, 1 - c, x, y))

        lower_of(k)
    for d in (0, 1, 3, 2):
        x_ = turn(x, d, NX)
        k = x_ * NC + 1 - c

        @pl.when(jnp.logical_not(in_plane))
        def _(x_=x_, k=k):
            arrived(column_v.at[rows_of(k * PIECE, PIECE)], r2.at[x_])

        lower_of(k)

    def product(start, size):
        part = jnp.dot(
            split_v[pl.ds(pl.multiple_of(start, 128), size), :], weights_v[...],
            preferred_element_type=jnp.float32,
        )
        return part[:, 0:STRIP] + part[:, STRIP:]

    for half in range(2):
        part_v[half, EDGE:HALF] = product(half * HALF + EDGE, HALF - EDGE)
    for e in Y_FAR:
        y_ = turn(y, e, NY)
        send(part_v.at[:, rows_of(EDGE + y_ * 2 * REST, 2 * REST)], yin2_v.at[e], sy2.at[e], ry2.at[e], at(z, c, x, y_))
    for d in X_FAR + (0,):
        x_ = turn(x, d, NX)
        half, start = x_ // 2, lax.rem(x_, 2) * PART
        part_v[half, rows_of(start, PART), :] = product(half * HALF + start, PART)
        if d:
            for e in Y_FAR + (0,):
                y_ = turn(y, e, NY)
                k = (d - 1) * NY + e
                send(part_v.at[half, rows_of(start + y_ * MAIN, MAIN)], xin_v.at[d - 1, e], sx.at[k], rx.at[k], at(z, c, x_, y))

    mine, low_x = x // 2, lax.rem(x, 2)
    kept = None
    for i, e in enumerate(Y_FAR + (0,)):
        if i == 3:
            total = back_v[c, z]
            for d in range(1, NZ):
                arrived(backs_v.at[d], rb.at[d])
                total = total + backs_v[d]
            backsum_v[...] = total
            target = lax.rem(col, 2) * pieces + z * NC + (1 - c)
            send(backsum_v, backin_v, sf.at[0], rf.at[0], (col // 2, target))
        if i == 6:
            total = part_v[:, rows_of(EDGE + y * 2 * REST, 2 * REST), :]
            for d in range(1, NY):
                arrived(yin2_v.at[d], ry2.at[d])
                total = total + yin2_v[d]
            xsend2_v[...] = total
            for d in X_FAR:
                x_ = turn(x, d, NX)
                src = xsend2_v.at[x_ // 2, rows_of(lax.rem(x_, 2) * REST, REST)]
                send(src, xin2_v.at[d], sx2.at[d], rx2.at[d], at(z, c, x_, y))
        y_ = turn(y, e, NY)
        total = part_v[mine, rows_of(low_x * PART + y_ * MAIN, MAIN), :]
        for d in range(1, NX):
            k = (d - 1) * NY + e
            arrived(xin_v.at[d - 1, e], rx.at[k])
            total = total + xin_v[d - 1, e]
        if e:
            ysend_v[e] = total
            send(ysend_v.at[e], yin_v.at[e], sy.at[e], ry.at[e], at(z, c, x, y_))
        else:
            kept = total
    rest = xsend2_v[mine, rows_of(low_x * REST, REST), :]
    for d in range(1, NX):
        arrived(xin2_v.at[d], rx2.at[d])
        rest = rest + xin2_v[d]
    for e in range(1, NY):
        arrived(yin_v.at[e], ry.at[e])
        kept = kept + yin_v[e]
    kept = jnp.concatenate([kept, rest], axis=0)
    arrived(backin_v, rf.at[0])
    done = -exact(kept + backin_v[...], unit_v[...])

    def main_rows(x_, y_):
        return out_v.at[x_ // 2, rows_of(lax.rem(x_, 2) * PART + y_ * MAIN, MAIN)]

    def rest_rows(x_, y_):
        return out_v.at[x_ // 2, rows_of(EDGE + y_ * 2 * REST + lax.rem(x_, 2) * REST, REST)]

    def rest_part(y_):
        return out_v.at[:, rows_of(EDGE + y_ * 2 * REST, 2 * REST)]

    main_rows(x, y)[...] = done[0:MAIN]
    rest_rows(x, y)[...] = done[MAIN:]
    for d in X_FAR:
        send(rest_rows(x, y), rest_rows(x, y), sxg2.at[d], rxg2.at[d], at(z, c, turn(x, d, NX), y))
    for e in Y_FAR:
        send(main_rows(x, y), main_rows(x, y), syg.at[e], ryg.at[e], at(z, c, x, turn(y, e, NY)))

    for e in (0,) + Y_NEAR:
        block = main_rows(x, turn(y, NY - e, NY))
        if e:
            arrived(block, ryg.at[e])
        for d in X_FAR:
            k = (d - 1) * NY + e
            send(block, block, sxg.at[k], rxg.at[k], at(z, c, turn(x, d, NX), y))
        if e == 1:
            for d in range(1, NX):
                arrived(rest_rows(turn(x, NX - d, NX), y), rxg2.at[d])
            for d in Y_FAR:
                send(rest_part(y), rest_part(y), syg2.at[d], ryg2.at[d], at(z, c, x, turn(y, d, NY)))

    for d in range(1, NX):
        for e in range(NY):
            arrived(main_rows(turn(x, NX - d, NX), turn(y, NY - e, NY)), rxg.at[(d - 1) * NY + e])
    for e in range(1, NY):
        arrived(rest_part(turn(y, NY - e, NY)), ryg2.at[e])

    def left_here(ref, sem):
        pltpu.make_async_copy(ref, ref, sem).wait()

    @pl.when(is_source)
    def _():
        for i in range((NZ - 1) * NC):
            left_here(column_v.at[pl.ds(0, PIECE)], s1.at[i])

    @pl.when(has_block)
    def _():
        left_here(column_v, s3.at[0])

    @pl.when(jnp.logical_not(in_plane))
    def _():
        for d in range(NX):
            left_here(column_v.at[pl.ds(0, PIECE)], s2.at[d])

    left_here(pairin_v, sp.at[0])
    for d in range(1, NZ):
        left_here(backs_v.at[d], sb.at[d])
    left_here(backsum_v, sf.at[0])
    for k in range((NX - 1) * NY):
        left_here(xin_v.at[0, 0], sx.at[k])
        left_here(xin_v.at[0, 0], sxg.at[k])
    for e in range(1, NY):
        left_here(yin_v.at[e], sy.at[e])
        left_here(yin_v.at[e], syg.at[e])
        left_here(yin2_v.at[e], sy2.at[e])
        left_here(yin2_v.at[e], syg2.at[e])
    for d in range(1, NX):
        left_here(xin2_v.at[d], sx2.at[d])
        left_here(xin2_v.at[d], sxg2.at[d])


def shards(strip, below, first, second, cotangent):
    f32, bf16 = jnp.float32, jnp.bfloat16
    dma = pltpu.SemaphoreType.DMA
    main = (NX - 1) * NY
    pairs = (
        (NZ - 1) * NC, NX, NX, NX, 1, 1, 1, 1, NZ, NZ, 1, 1,
        main, main, NY, NY, NY, NY, main, main,
        NY, NY, NX, NX, NX, NX, NY, NY,
    )
    out = pl.pallas_call(
        kernel,
        out_shape=pltpu.VMEM((2, HALF, STRIP), f32),
        in_specs=[pl.BlockSpec(memory_space=pltpu.HBM)] * 5,
        out_specs=pl.BlockSpec(memory_space=pltpu.VMEM),
        scratch_shapes=[
            pltpu.VMEM((ROWS, STRIP), f32),
            pltpu.VMEM((PANEL, PANEL), f32),
            pltpu.VMEM((PANEL, PANEL), f32),
            pltpu.VMEM((PANEL, PANEL), f32),
            pltpu.VMEM((ROWS, COLS), f32),
            pltpu.VMEM((ROWS, 2 * COLS), bf16),
            pltpu.VMEM((COLS, STRIP), f32),
            pltpu.VMEM((2 * COLS, 2 * STRIP), bf16),
            pltpu.VMEM((NC, NZ, SUB, STRIP), f32),
            pltpu.VMEM((NZ, SUB, STRIP), f32),
            pltpu.VMEM((NZ, SUB, STRIP), f32),
            pltpu.VMEM((SUB, STRIP), f32),
            pltpu.VMEM((SUB, STRIP), f32),
            pltpu.VMEM((2, HALF, STRIP), f32),
            pltpu.VMEM((NX - 1, NY, MAIN, STRIP), f32),
            pltpu.VMEM((NY, MAIN, STRIP), f32),
            pltpu.VMEM((NY, MAIN, STRIP), f32),
            pltpu.VMEM((NY, 2, 2 * REST, STRIP), f32),
            pltpu.VMEM((2, 2 * REST, STRIP), f32),
            pltpu.VMEM((NX, REST, STRIP), f32),
            pltpu.VMEM((STRIP, STRIP), f32),
            dma((4 + C_CHUNKS,)),
            pltpu.SemaphoreType.REGULAR,
        ] + [dma((n,)) for n in pairs],
        compiler_params=pltpu.CompilerParams(
            collective_id=0, has_side_effects=True, vmem_limit_bytes=40 << 20,
        ),
    )(*[pltpu.with_memory_space_constraint(v, pltpu.HBM) for v in (strip, below, first, second, cotangent)])
    return out.reshape(ROWS, STRIP)


def solution(mesh):
    return jax.shard_map(
        shards,
        mesh=mesh,
        in_specs=(P("row", None), P(), P(), P(), P("row", "col")),
        out_specs=P("row", None),
        check_vma=False,
    )
```

```python
import jax
import jax.numpy as jnp
from jax import lax
from jax.experimental import pallas as pl
from jax.experimental.pallas import tpu as pltpu
from jax.sharding import PartitionSpec as P

MESH = pl.DeviceIdType.MESH
NX, NY, NZ, NC = 4, 8, 8, 2
ROWS, COLS, STRIP, PANEL = 1280, 640, 128, 64
HALF = ROWS // 2
MAIN, REST = 32, 8
SUB = MAIN + REST
PART = MAIN * NY
EDGE = PART * 2
PIECE = COLS // NX // NC
Y_FAR = (4, 3, 5, 2, 6, 1, 7)
Y_NEAR = (1, 7, 2, 6, 3, 5, 4)
X_FAR = (2, 1, 3)
Z_FAR = (4, 3, 5, 2, 6, 1, 7)
C_CHUNKS = 5


def exact(left, right, dims=((1,), (0,))):
    return lax.dot_general(
        left, right, (dims, ((), ())),
        precision=lax.Precision.HIGHEST, preferred_element_type=jnp.float32,
    )


def halves(value):
    high = value.astype(jnp.bfloat16)
    low = (value - high.astype(jnp.float32)).astype(jnp.bfloat16)
    return high, low


def rows_of(start, size):
    return pl.ds(pl.multiple_of(start, 8), size)


def kernel(
    strip_h, below_h, first_h, second_h, cot_h, out_v,
    strip_v, below_v, first_v, second_v, cot_v, split_v, column_v, weights_v,
    back_v, pairin_v, backs_v, backsum_v, backin_v,
    part_v, xin_v, ysend_v, yin_v, yin2_v, xsend2_v, xin2_v, unit_v,
    load_sem, peer_sem,
    s1, r1, s2, r2, s3, r3, sp, rp, sb, rb, sf, rf, sx, rx, sy, ry, syg, ryg, sxg, rxg,
    sy2, ry2, sx2, rx2, sxg2, rxg2, syg2, ryg2,
):
    row, col = lax.axis_index("row"), lax.axis_index("col")
    z, c = row // NC, row % NC
    x, y = col // NY, col % NY

    def at(z_, c_, x_, y_):
        return (z_ * NC + c_, x_ * NY + y_)

    def send(src, dst, ssem, rsem, device):
        copy = pltpu.make_async_remote_copy(
            src_ref=src, dst_ref=dst, send_sem=ssem, recv_sem=rsem,
            device_id=device, device_id_type=MESH,
        )
        copy.start()
        return copy

    def arrived(dst, rsem):
        pltpu.make_async_copy(dst, dst, rsem).wait()

    def turn(base, d, n):
        return lax.rem(base + d, n)

    is_source = (y // 2) == lax.rem(row, 4)
    target_x = row // 4
    source_rows = lax.rem(y, 2) * COLS
    in_plane = (2 * x + y // 4) == z
    has_block = jnp.logical_and(in_plane, lax.rem(y // 2, NC) == c)

    barrier = pltpu.get_barrier_semaphore()

    def greet(peer):
        pl.semaphore_signal(barrier, inc=1, device_id=peer, device_id_type=MESH)

    @pl.when(jnp.logical_not(in_plane))
    def _():
        for x_ in range(NX):
            greet(at(2 * x + y // 4, lax.rem(y // 2, NC), x_, y))

    peers = [at(z, 1 - c, x, y)]
    peers += [at(turn(z, d, NZ), c, x, y) for d in Z_FAR]
    peers += [at(z, c, x, turn(y, d, NY)) for d in Y_FAR]
    peers += [at(z, c, turn(x, d, NX), y) for d in X_FAR]
    for peer in peers:
        greet(peer)

    small = []
    for i, (src, dst) in enumerate(((below_h, below_v), (first_h, first_v), (second_h, second_v), (strip_h, strip_v))):
        copy = pltpu.make_async_copy(src, dst, load_sem.at[i])
        copy.start()
        small.append(copy)
    chunk = ROWS // C_CHUNKS
    loads = []
    for i in range(C_CHUNKS):
        rows = pl.ds(i * chunk, chunk)
        copy = pltpu.make_async_copy(cot_h.at[rows], cot_v.at[rows], load_sem.at[4 + i])
        copy.start()
        loads.append(copy)

    pl.semaphore_wait(barrier, len(peers) + jnp.where(is_source, (NZ - 1) * NC, 0))
    for d in range(1, NX):
        pl.semaphore_signal(peer_sem, inc=1, device_id=at(z, c, turn(x, d, NX), y), device_id_type=MESH)

    small[3].wait()

    @pl.when(is_source)
    def _():
        for i, d in enumerate(Z_FAR):
            for h in range(NC):
                src = strip_v.at[rows_of(source_rows + (x * NC + h) * PIECE, PIECE)]
                dst = column_v.at[rows_of((x * NC + h) * PIECE, PIECE)]
                send(src, dst, s1.at[i * NC + h], r1.at[x], at(turn(z, d, NZ), h, target_x, y))

    @pl.when(has_block)
    def _():
        send(strip_v.at[rows_of(source_rows, COLS)], column_v, s3.at[0], r3.at[0], at(z, 1 - c, x, y))

    for copy in small[:3]:
        copy.wait()
    first, second = first_v[...], second_v[...]
    left = exact(below_v[...], first, ((1,), (1,)))
    mixed = exact(exact(second, left), first)
    unit_v[0:PANEL, 0:PANEL] = first
    unit_v[0:PANEL, PANEL:] = jnp.zeros_like(first)
    unit_v[PANEL:, 0:PANEL] = -mixed
    unit_v[PANEL:, PANEL:] = second

    for i in range(C_CHUNKS):
        loads[i].wait()
        rows = pl.ds(i * chunk, chunk)
        high, low = halves(cot_v[rows, :])
        split_v[rows, 0:COLS] = high
        split_v[rows, COLS:] = low

    def piece_y(z_):
        return lax.rem(y + z_ + (NZ + 4) - (2 * x + y // 4), NY)

    high, low = halves(jnp.transpose(exact(strip_v[...], unit_v[...], ((1,), (1,)))))
    back = jnp.dot(jnp.concatenate([high, low], axis=0), split_v[...], preferred_element_type=jnp.float32)
    back = back[0:STRIP] + back[STRIP:]
    back = jnp.transpose(back[:, 0:COLS] + back[:, COLS:])
    pieces = NZ * NC
    for k in range(pieces):
        rest = pieces * MAIN + (k % NY * 2 + k // NY) * REST
        back_v[k // NY, k % NY, 0:MAIN] = back[k * MAIN:(k + 1) * MAIN]
        back_v[k // NY, k % NY, MAIN:] = back[rest:rest + REST]
    pl.semaphore_wait(peer_sem, NX - 1)
    send(back_v.at[1 - c], pairin_v, sp.at[0], rp.at[0], at(z, 1 - c, x, y))

    arrived(pairin_v, rp.at[0])
    back_v[c] = back_v[c] + pairin_v[...]
    for d in Z_FAR:
        z_ = turn(z, d, NZ)
        send(back_v.at[c, piece_y(z_)], backs_v.at[d], sb.at[d], rb.at[d], at(z_, c, x, y))

    @pl.when(has_block)
    def _():
        column_v[...] = strip_v[rows_of(source_rows, COLS), :]

    @pl.when(jnp.logical_and(in_plane, jnp.logical_not(has_block)))
    def _():
        arrived(column_v, r3.at[0])

    def lower_of(k):
        start = k * PIECE
        high, low = halves(exact(column_v[rows_of(start, PIECE), :], unit_v[...], ((1,), (1,))))
        both = jnp.concatenate([high, low], axis=1)
        weights_v[pl.ds(pl.multiple_of(start, 16), PIECE), :] = both
        weights_v[pl.ds(pl.multiple_of(COLS + start, 16), PIECE), :] = both

    for d in (0, 1, 3, 2):
        x_ = turn(x, d, NX)
        k = x_ * NC + c

        @pl.when(jnp.logical_not(in_plane))
        def _(d=d, x_=x_, k=k):
            block = column_v.at[rows_of(k * PIECE, PIECE)]
            arrived(block, r1.at[x_])
            send(block, block, s2.at[d], r2.at[x_], at(z, 1 - c, x, y))

        lower_of(k)
    for d in (0, 1, 3, 2):
        x_ = turn(x, d, NX)
        k = x_ * NC + 1 - c

        @pl.when(jnp.logical_not(in_plane))
        def _(x_=x_, k=k):
            arrived(column_v.at[rows_of(k * PIECE, PIECE)], r2.at[x_])

        lower_of(k)

    def product(start, size):
        part = jnp.dot(
            split_v[pl.ds(pl.multiple_of(start, 128), size), :], weights_v[...],
            preferred_element_type=jnp.float32,
        )
        return part[:, 0:STRIP] + part[:, STRIP:]

    for half in range(2):
        part_v[half, EDGE:HALF] = product(half * HALF + EDGE, HALF - EDGE)
    for e in Y_FAR:
        y_ = turn(y, e, NY)
        send(part_v.at[:, rows_of(EDGE + y_ * 2 * REST, 2 * REST)], yin2_v.at[e], sy2.at[e], ry2.at[e], at(z, c, x, y_))
    for d in X_FAR + (0,):
        x_ = turn(x, d, NX)
        half, start = x_ // 2, lax.rem(x_, 2) * PART
        part_v[half, rows_of(start, PART), :] = product(half * HALF + start, PART)
    for e in Y_FAR + (0,):
        y_ = turn(y, e, NY)
        for d in X_FAR:
            x_ = turn(x, d, NX)
            k = (d - 1) * NY + e
            src = part_v.at[x_ // 2, rows_of(lax.rem(x_, 2) * PART + y_ * MAIN, MAIN)]
            send(src, xin_v.at[d - 1, e], sx.at[k], rx.at[k], at(z, c, x_, y))

    mine, low_x = x // 2, lax.rem(x, 2)
    kept = None
    for i, e in enumerate(Y_FAR + (0,)):
        if i == 1:
            total = back_v[c, piece_y(z)]
            for d in range(1, NZ):
                arrived(backs_v.at[d], rb.at[d])
                total = total + backs_v[d]
            backsum_v[...] = total
            send(backsum_v, backin_v, sf.at[0], rf.at[0], at(2 * x + y // 4, lax.rem(y // 2, NC), lax.rem(y, 2) * 2 + c, piece_y(z)))
        if i == 6:
            total = part_v[:, rows_of(EDGE + y * 2 * REST, 2 * REST), :]
            for d in range(1, NY):
                arrived(yin2_v.at[d], ry2.at[d])
                total = total + yin2_v[d]
            xsend2_v[...] = total
            for d in X_FAR:
                x_ = turn(x, d, NX)
                src = xsend2_v.at[x_ // 2, rows_of(lax.rem(x_, 2) * REST, REST)]
                send(src, xin2_v.at[d], sx2.at[d], rx2.at[d], at(z, c, x_, y))
        y_ = turn(y, e, NY)
        total = part_v[mine, rows_of(low_x * PART + y_ * MAIN, MAIN), :]
        for d in range(1, NX):
            k = (d - 1) * NY + e
            arrived(xin_v.at[d - 1, e], rx.at[k])
            total = total + xin_v[d - 1, e]
        if e:
            ysend_v[e] = total
            send(ysend_v.at[e], yin_v.at[e], sy.at[e], ry.at[e], at(z, c, x, y_))
        else:
            kept = total
    rest = xsend2_v[mine, rows_of(low_x * REST, REST), :]
    for d in range(1, NX):
        arrived(xin2_v.at[d], rx2.at[d])
        rest = rest + xin2_v[d]
    for e in range(1, NY):
        arrived(yin_v.at[e], ry.at[e])
        kept = kept + yin_v[e]
    kept = jnp.concatenate([kept, rest], axis=0)
    arrived(backin_v, rf.at[0])
    done = -exact(kept + backin_v[...], unit_v[...])

    def main_rows(x_, y_):
        return out_v.at[x_ // 2, rows_of(lax.rem(x_, 2) * PART + y_ * MAIN, MAIN)]

    def rest_rows(x_, y_):
        return out_v.at[x_ // 2, rows_of(EDGE + y_ * 2 * REST + lax.rem(x_, 2) * REST, REST)]

    def rest_part(y_):
        return out_v.at[:, rows_of(EDGE + y_ * 2 * REST, 2 * REST)]

    main_rows(x, y)[...] = done[0:MAIN]
    rest_rows(x, y)[...] = done[MAIN:]
    for d in X_FAR:
        send(rest_rows(x, y), rest_rows(x, y), sxg2.at[d], rxg2.at[d], at(z, c, turn(x, d, NX), y))
    for e in Y_FAR:
        send(main_rows(x, y), main_rows(x, y), syg.at[e], ryg.at[e], at(z, c, x, turn(y, e, NY)))

    for e in (0,) + Y_NEAR:
        block = main_rows(x, turn(y, NY - e, NY))
        if e:
            arrived(block, ryg.at[e])
        for d in X_FAR:
            k = (d - 1) * NY + e
            send(block, block, sxg.at[k], rxg.at[k], at(z, c, turn(x, d, NX), y))
        if e == 1:
            for d in range(1, NX):
                arrived(rest_rows(turn(x, NX - d, NX), y), rxg2.at[d])
            for d in Y_FAR:
                send(rest_part(y), rest_part(y), syg2.at[d], ryg2.at[d], at(z, c, x, turn(y, d, NY)))

    for d in range(1, NX):
        for e in range(NY):
            arrived(main_rows(turn(x, NX - d, NX), turn(y, NY - e, NY)), rxg.at[(d - 1) * NY + e])
    for e in range(1, NY):
        arrived(rest_part(turn(y, NY - e, NY)), ryg2.at[e])

    def left_here(ref, sem):
        pltpu.make_async_copy(ref, ref, sem).wait()

    @pl.when(is_source)
    def _():
        for i in range((NZ - 1) * NC):
            left_here(column_v.at[pl.ds(0, PIECE)], s1.at[i])

    @pl.when(has_block)
    def _():
        left_here(column_v, s3.at[0])

    @pl.when(jnp.logical_not(in_plane))
    def _():
        for d in range(NX):
            left_here(column_v.at[pl.ds(0, PIECE)], s2.at[d])

    left_here(pairin_v, sp.at[0])
    for d in range(1, NZ):
        left_here(backs_v.at[d], sb.at[d])
    left_here(backsum_v, sf.at[0])
    for k in range((NX - 1) * NY):
        left_here(xin_v.at[0, 0], sx.at[k])
        left_here(xin_v.at[0, 0], sxg.at[k])
    for e in range(1, NY):
        left_here(yin_v.at[e], sy.at[e])
        left_here(yin_v.at[e], syg.at[e])
        left_here(yin2_v.at[e], sy2.at[e])
        left_here(yin2_v.at[e], syg2.at[e])
    for d in range(1, NX):
        left_here(xin2_v.at[d], sx2.at[d])
        left_here(xin2_v.at[d], sxg2.at[d])


def shards(strip, below, first, second, cotangent):
    f32, bf16 = jnp.float32, jnp.bfloat16
    dma = pltpu.SemaphoreType.DMA
    main = (NX - 1) * NY
    pairs = (
        (NZ - 1) * NC, NX, NX, NX, 1, 1, 1, 1, NZ, NZ, 1, 1,
        main, main, NY, NY, NY, NY, main, main,
        NY, NY, NX, NX, NX, NX, NY, NY,
    )
    out = pl.pallas_call(
        kernel,
        out_shape=pltpu.VMEM((2, HALF, STRIP), f32),
        in_specs=[pl.BlockSpec(memory_space=pltpu.HBM)] * 5,
        out_specs=pl.BlockSpec(memory_space=pltpu.VMEM),
        scratch_shapes=[
            pltpu.VMEM((ROWS, STRIP), f32),
            pltpu.VMEM((PANEL, PANEL), f32),
            pltpu.VMEM((PANEL, PANEL), f32),
            pltpu.VMEM((PANEL, PANEL), f32),
            pltpu.VMEM((ROWS, COLS), f32),
            pltpu.VMEM((ROWS, 2 * COLS), bf16),
            pltpu.VMEM((COLS, STRIP), f32),
            pltpu.VMEM((2 * COLS, 2 * STRIP), bf16),
            pltpu.VMEM((NC, NY, SUB, STRIP), f32),
            pltpu.VMEM((NZ, SUB, STRIP), f32),
            pltpu.VMEM((NZ, SUB, STRIP), f32),
            pltpu.VMEM((SUB, STRIP), f32),
            pltpu.VMEM((SUB, STRIP), f32),
            pltpu.VMEM((2, HALF, STRIP), f32),
            pltpu.VMEM((NX - 1, NY, MAIN, STRIP), f32),
            pltpu.VMEM((NY, MAIN, STRIP), f32),
            pltpu.VMEM((NY, MAIN, STRIP), f32),
            pltpu.VMEM((NY, 2, 2 * REST, STRIP), f32),
            pltpu.VMEM((2, 2 * REST, STRIP), f32),
            pltpu.VMEM((NX, REST, STRIP), f32),
            pltpu.VMEM((STRIP, STRIP), f32),
            dma((4 + C_CHUNKS,)),
            pltpu.SemaphoreType.REGULAR,
        ] + [dma((n,)) for n in pairs],
        compiler_params=pltpu.CompilerParams(
            collective_id=0, has_side_effects=True, vmem_limit_bytes=40 << 20,
        ),
    )(*[pltpu.with_memory_space_constraint(v, pltpu.HBM) for v in (strip, below, first, second, cotangent)])
    return out.reshape(ROWS, STRIP)


def solution(mesh):
    return jax.shard_map(
        shards,
        mesh=mesh,
        in_specs=(P("row", None), P(), P(), P(), P("row", "col")),
        out_specs=P("row", None),
        check_vma=False,
    )
```
